32 devices in a mesh: uly: 8 (over z, y), blk: 4 (over x, core).
Axes of the slice: x: 2, y: 2, z: 4, core: 2. Of those that a mesh axis runs over, the one named last changes fastest.
Arguments:
- queries: bfloat16 [4096, 4096], P(('blk', 'uly')), may hold values from -8 to 8
- keys: bfloat16 [4096, 1024], P(('blk', 'uly')), may hold values from -8 to 8
- values: bfloat16 [4096, 1024], P(('blk', 'uly')), may hold values from -6 to 6
- live_blocks: int32 [32, 8], replicated, may hold values from 0 to 31, as said below
Outputs:
- attended: bfloat16 [4096, 4096], P(('blk', 'uly'))
The draws below stay inside these ranges and needn't reach their ends.
Inputs may be any that keep to these rules, and one draw needn't show every extreme that they name: `live_blocks`: each row holds 8 different block numbers, among them the row's own block, the blocks just before and after it where they exist, and block 0; the others are drawn from the seed.
All inputs are finite; a program needn't handle non-finite values.
Results may differ from the reference program's by a relative error of at most 0.0049.
Values may be sent and summed in bfloat16 or wider, within the bound.
A program may use at most 128 MiB of HBM per device.

```python
import math
import jax
import jax.numpy as jnp
from jax import lax

H = 32
KVH = 8
HD = 128
BLOCK = 128
LIVE = 8
TOKENS = 4096
NB = 32


def drawn_part(key, shape):
    return jax.random.truncated_normal(key, -6.0, 6.0, shape, jnp.float32)


def draw_queries(key, part):
    shape = (TOKENS, H * HD)
    result = drawn_part(jax.random.fold_in(key, 21), shape)
    return result.astype(jnp.bfloat16)


def draw_keys(key, part):
    shape = (TOKENS, KVH * HD)
    result = drawn_part(jax.random.fold_in(key, 22), shape)
    return result.astype(jnp.bfloat16)


def draw_live_blocks(key, part):
    row_ids = jnp.arange(NB, dtype=jnp.int32)[:, None]
    col_ids = jnp.arange(NB, dtype=jnp.int32)[None, :]
    noise = jax.random.randint(jax.random.fold_in(key, 31), (NB, NB), 0, 65536, dtype=jnp.int32)
    forced = (jnp.abs(col_ids - row_ids) <= 1) | (col_ids == 0)
    priority = noise * NB + col_ids + jnp.where(forced, 1 << 28, 0)
    return lax.top_k(priority, LIVE)[1].astype(jnp.int32)


def block_levels(own_key, extent, cuts, least, largest):
    def one(axis_at, shards_of):
        draws = jax.random.uniform(jax.random.fold_in(jax.random.fold_in(own_key, 6), axis_at), (shards_of,), jnp.float32, least / len(cuts), largest / len(cuts))
        return jnp.repeat(jnp.exp(draws), extent[axis_at] // shards_of).reshape((-1,) + (1,) * (len(extent) - axis_at - 1))

    factor_of = one(*cuts[0])
    for cut in cuts[1:]:
        factor_of = factor_of * one(*cut)
    return factor_of


def bell_draw(rng, extent, scale, reach, cuts=(), kind=jnp.bfloat16):
    entries = jax.random.normal(rng, extent, jnp.float32) * scale
    if len(cuts) > 0:
        entries = block_levels(rng, extent, cuts, -0.22, 0.18) * entries
    return jnp.clip(entries, min=-reach, max=reach).astype(kind)


def setup_inputs(seed: int = 0) -> dict:
    arg_keys = jax.random.split(jax.random.key(seed), 5)
    queries = draw_queries(jax.random.fold_in(arg_keys[4], 71), 0)
    keys = draw_keys(jax.random.fold_in(arg_keys[4], 71), 0)
    values = bell_draw(arg_keys[2], (TOKENS, KVH * HD), 1.0, 6.0, ((0, 32),))
    live_blocks = draw_live_blocks(jax.random.fold_in(arg_keys[4], 71), 0)
    return dict(queries=queries, keys=keys, values=values, live_blocks=live_blocks)


def reference(queries, keys, values, live_blocks):
    share = H // KVH
    score_scale = 1.0 / math.sqrt(HD)
    query_blocks = queries.reshape(NB, BLOCK, KVH, share, HD)
    key_blocks = keys.reshape(NB, BLOCK, KVH, HD)
    value_blocks = values.reshape(NB, BLOCK, KVH, HD)

    def attend_block(block_index):
        live_rows = live_blocks[block_index]
        query_block = query_blocks[block_index].astype(jnp.float32)
        key_rows = key_blocks[live_rows].astype(jnp.float32)
        value_rows = value_blocks[live_rows].astype(jnp.float32)
        scores = jnp.einsum('qgrd,lkgd->qgrlk', query_block, key_rows) * score_scale
        row_max = lax.optimization_barrier(jnp.max(scores, axis=(3, 4), keepdims=True))
        weights = jnp.exp(scores - row_max)
        denominator = lax.optimization_barrier(jnp.sum(weights, axis=(3, 4)))
        rounded = lax.optimization_barrier(weights.astype(jnp.bfloat16))
        numerator = jnp.einsum('qgrlk,lkgd->qgrd', rounded.astype(jnp.float32), value_rows)
        return (numerator / denominator[..., None]).astype(jnp.bfloat16)
    attended = lax.map(attend_block, jnp.arange(NB, dtype=jnp.int32))
    return attended.reshape(TOKENS, H * HD)
```

```python
import math

import jax
import jax.numpy as jnp
from jax import lax
from jax.experimental import pallas as pl
from jax.experimental.pallas import tpu as pltpu
from jax.sharding import PartitionSpec as P

HD = 128
CORES = 2
SIDE = 2
GROUP = SIDE * SIDE * CORES
MESH = pl.DeviceIdType.MESH


class Layout:
    def __init__(self, n_uly, n_blk):
        self.n_uly = n_uly
        self.nx = n_blk // CORES
        self.ny = 2 ** (int(math.log2(n_uly)) // 2)
        self.nz = n_uly // self.ny
        self.columns = n_uly * n_blk // GROUP

    def split(self, uly, blk):
        x, core = blk // CORES, blk % CORES
        z, y = uly // self.ny, uly % self.ny
        column = ((x // SIDE) * (self.ny // SIDE) + y // SIDE) * self.nz + z
        member = ((x % SIDE) * SIDE + y % SIDE) * CORES + core
        return column, member

    def join(self, column, member):
        z, square = column % self.nz, column // self.nz
        x = (square // (self.ny // SIDE)) * SIDE + member // (SIDE * CORES)
        y = (square % (self.ny // SIDE)) * SIDE + (member // CORES) % SIDE
        return z * self.ny + y, x * CORES + member % CORES

    def slot(self, block):
        column, member = self.split(block % self.n_uly, block // self.n_uly)
        return column * GROUP + member


def partner(member, rel):
    a = (member // 4 + rel // 4) % 2
    b = ((member // 2) % 2 + (rel // 2) % 2) % 2
    c = (member % 2 + rel % 2) % 2
    return a * 4 + b * 2 + c


def kernel(lay, live_ref, q_ref, k_ref, v_ref, o_ref,
           qbuf, kbuf, vbuf, pbuf, lbuf, obuf,
           plane_send, plane_recv, own_sem, relay_send, k_recv, v_recv, o_send, o_recv):
    width = q_ref.shape[1] // GROUP
    share = width // HD
    live = live_ref.shape[1]
    last = lay.columns - 1
    column, member = lay.split(lax.axis_index("uly"), lax.axis_index("blk"))

    def device(col, mem):
        uly, blk = lay.join(col, mem)
        return {"uly": uly, "blk": blk}

    has_down, has_up = column > 0, column < last
    down, up = jnp.maximum(column - 1, 0), jnp.minimum(column + 1, last)

    barrier = pltpu.get_barrier_semaphore()
    for rel in range(1, GROUP):
        pl.semaphore_signal(barrier, inc=1, device_id=device(column, partner(member, rel)), device_id_type=MESH)

    @pl.when(has_down)
    def _():
        pl.semaphore_signal(barrier, inc=1, device_id=device(down, member), device_id_type=MESH)

    @pl.when(has_up)
    def _():
        pl.semaphore_signal(barrier, inc=1, device_id=device(up, member), device_id_type=MESH)

    def cols(index, size):
        return pl.ds(pl.multiple_of(index * size, size), size)

    here = column * GROUP + member
    own = [
        pltpu.make_async_copy(k_ref.at[:, cols(member, HD)], kbuf.at[here], own_sem.at[0]),
        pltpu.make_async_copy(v_ref.at[:, cols(member, HD)], vbuf.at[here], own_sem.at[1]),
        pltpu.make_async_copy(q_ref.at[:, cols(member, width)], qbuf.at[0], own_sem.at[2]),
    ]
    for copy in own:
        copy.start()
    arrivals = 7 + has_down.astype(jnp.int32) + has_up.astype(jnp.int32)
    pl.semaphore_wait(barrier, arrivals)

    def plane(kind, rel, source_member=None):
        other = partner(member, rel)
        src, dst, size = (
            (k_ref, kbuf.at[here], HD),
            (v_ref, vbuf.at[here], HD),
            (q_ref, qbuf.at[rel], width),
        )[kind]
        return pltpu.make_async_remote_copy(
            src.at[:, cols(other, size)], dst, plane_send.at[kind, rel], plane_recv.at[kind, rel],
            device_id=device(column, other), device_id_type=MESH,
        )

    for kind in range(3):
        for rel in range(1, GROUP):
            plane(kind, rel).start()

    def hop(kind, way, col, item):
        buf, recv = ((kbuf, k_recv), (vbuf, v_recv))[kind]
        index = col * GROUP + item
        return pltpu.make_async_remote_copy(
            buf.at[index], buf.at[index], relay_send.at[kind, way, col], recv.at[index],
            device_id=device((down, up)[way], member), device_id_type=MESH,
        )

    def forward(kind, way, col, item):
        @pl.when((has_down, has_up)[way])
        def _():
            hop(kind, way, col, item).start()

    for kind in range(2):
        for rel in range(GROUP):
            if rel == 0:
                own[kind].wait()
            else:
                plane(kind, rel).wait_recv()
            forward(kind, 0, column, partner(member, rel))
            forward(kind, 1, column, partner(member, rel))

    @pl.loop(1, lay.columns)
    def _(step):
        above, below = column + step, column - step
        for kind in range(2):
            @pl.loop(0, GROUP)
            def _(item):
                @pl.when((above <= last) if kind == 0 else ((above <= last) & has_down))
                def _():
                    hop(kind, 0, above, item).wait_recv()
                    forward(kind, 0, above, item)

                @pl.when((below >= 0) if kind == 0 else ((below >= 0) & has_up))
                def _():
                    hop(kind, 1, below, item).wait_recv()
                    forward(kind, 1, below, item)

    own[2].wait()
    for rel in range(1, GROUP):
        plane(2, rel).wait_recv()

    factor = math.log2(math.e) / math.sqrt(HD)

    def block_of(rel):
        uly, blk = lay.join(column, partner(member, rel))
        return blk * lay.n_uly + uly

    def picked(buf, rel):
        block = block_of(rel)
        return jnp.concatenate([buf[lay.slot(live_ref[block, i])] for i in range(live)], axis=0)

    @pl.loop(0, GROUP)
    def _(rel):
        queries = jnp.concatenate([qbuf[rel, :, r * HD:(r + 1) * HD] for r in range(share)], axis=0)
        scores = lax.dot_general(
            queries, picked(kbuf, rel), (((1,), (1,)), ((), ())), preferred_element_type=jnp.float32
        )
        row_max = jnp.max(scores, axis=1, keepdims=True)
        weights = jnp.exp2((scores - row_max) * factor)
        total = jnp.sum(weights, axis=1, keepdims=True)
        lbuf[rel] = jnp.broadcast_to(total, lbuf.shape[1:])
        pbuf[rel] = weights.astype(jnp.bfloat16)

    @pl.loop(1, lay.columns)
    def _(step):
        above, below = column + step, column - step

        @pl.loop(0, GROUP)
        def _(item):
            @pl.when((above <= last) & jnp.logical_not(has_down))
            def _():
                hop(1, 0, above, item).wait_recv()

            @pl.when((below >= 0) & jnp.logical_not(has_up))
            def _():
                hop(1, 1, below, item).wait_recv()

    def back(rel):
        other = partner(member, rel)
        return pltpu.make_async_remote_copy(
            obuf.at[rel], o_ref.at[:, cols(member, width)], o_send.at[rel], o_recv.at[rel],
            device_id=device(column, other), device_id_type=MESH,
        )

    def attended(rel):
        product = jnp.dot(pbuf[rel], picked(vbuf, rel), preferred_element_type=jnp.float32)
        result = (product / lbuf[rel]).astype(jnp.bfloat16)
        rows = result.shape[0] // share
        return jnp.concatenate([result[r * rows:(r + 1) * rows] for r in range(share)], axis=1)

    @pl.loop(0, GROUP - 1)
    def _(step):
        rel = GROUP - 1 - step
        obuf[rel] = attended(rel)

        @pl.when(step > 0)
        def _():
            back(rel + 1).start()

    o_ref[:, cols(member, width)] = attended(0)
    back(1).start()

    for kind in range(3):
        for rel in range(1, GROUP):
            plane(kind, rel).wait_send()

    def sent(kind, way, col):
        buf = (kbuf, vbuf)[kind].at[pl.ds(col * GROUP, GROUP)]
        pltpu.make_async_copy(buf, buf, relay_send.at[kind, way, col]).wait()

    @pl.loop(0, lay.columns)
    def _(col):
        for kind in range(2):
            @pl.when((col >= column) & has_down)
            def _():
                sent(kind, 0, col)

            @pl.when((col <= column) & has_up)
            def _():
                sent(kind, 1, col)

    for rel in range(1, GROUP):
        back(rel).wait()


def solution(mesh):
    lay = Layout(mesh.shape["uly"], mesh.shape["blk"])

    def body(queries, keys, values, live_blocks):
        rows, hidden = queries.shape
        width = hidden // GROUP
        share = width // HD
        slots = lay.columns * GROUP
        keys_seen = live_blocks.shape[1] * rows
        bf16, f32 = jnp.bfloat16, jnp.float32
        dma = pltpu.SemaphoreType.DMA
        vmem = pl.BlockSpec(memory_space=pltpu.VMEM)

        def call(*refs):
            kernel(lay, *refs)

        return pl.pallas_call(
            call,
            out_shape=jax.ShapeDtypeStruct((rows, hidden), bf16),
            in_specs=[pl.BlockSpec(memory_space=pltpu.SMEM), vmem, vmem, vmem],
            out_specs=vmem,
            scratch_shapes=[
                pltpu.VMEM((GROUP, rows, width), bf16),
                pltpu.VMEM((slots, rows, HD), bf16),
                pltpu.VMEM((slots, rows, HD), bf16),
                pltpu.VMEM((GROUP, rows * share, keys_seen), bf16),
                pltpu.VMEM((GROUP, rows * share, HD), f32),
                pltpu.VMEM((GROUP, rows, width), bf16),
                dma((3, GROUP)),
                dma((3, GROUP)),
                dma((3,)),
                dma((2, 2, lay.columns)),
                dma((slots,)),
                dma((slots,)),
                dma((GROUP,)),
                dma((GROUP,)),
            ],
            compiler_params=pltpu.CompilerParams(
                collective_id=0, has_side_effects=True, vmem_limit_bytes=56 * 2**20
            ),
            name="group_attention",
        )(live_blocks, queries, keys, values)

    spec = P(("blk", "uly"), None)
    return jax.shard_map(
        body, mesh=mesh, in_specs=(spec, spec, spec, P()), out_specs=spec, check_vma=False
    )
```

```python
import math

import jax
import jax.numpy as jnp
from jax import lax
from jax.experimental import pallas as pl
from jax.experimental.pallas import tpu as pltpu
from jax.sharding import PartitionSpec as P

HD = 128
CORES = 2
SIDE = 2
CHIPS = SIDE * SIDE
GROUP = CHIPS * CORES
MESH = pl.DeviceIdType.MESH


class Layout:
    def __init__(self, n_uly, n_blk):
        self.n_uly = n_uly
        self.nx = n_blk // CORES
        self.ny = 2 ** (int(math.log2(n_uly)) // 2)
        self.nz = n_uly // self.ny
        self.columns = n_uly * n_blk // GROUP

    def split(self, uly, blk):
        x, core = blk // CORES, blk % CORES
        z, y = uly // self.ny, uly % self.ny
        column = ((x // SIDE) * (self.ny // SIDE) + y // SIDE) * self.nz + z
        return column, (x % SIDE) * SIDE + y % SIDE, core

    def join(self, column, chip, core):
        z, square = column % self.nz, column // self.nz
        x = (square // (self.ny // SIDE)) * SIDE + chip // SIDE
        y = (square % (self.ny // SIDE)) * SIDE + chip % SIDE
        return z * self.ny + y, x * CORES + core

    def slot(self, block):
        column, chip, core = self.split(block % self.n_uly, block // self.n_uly)
        return column * GROUP + core * CHIPS + chip


def partner(chip, rel):
    a = (chip // 2 + rel // 2) % 2
    b = (chip % 2 + rel % 2) % 2
    return a * 2 + b


def kernel(lay, live_ref, q_ref, k_ref, v_ref, o_ref,
           qbuf, ka, va, kb, vb, pbuf, lbuf, obuf,
           plane_send, plane_recv, own_sem, relay_send, recv, o_send, o_recv):
    heads = k_ref.shape[1] // HD // CHIPS
    width = q_ref.shape[1] // CHIPS // heads
    share = width // HD
    live = live_ref.shape[1]
    last = lay.columns - 1
    bufs = ((ka, va), (kb, vb))
    column, chip, core = lay.split(lax.axis_index("uly"), lax.axis_index("blk"))

    def device(col, which, core_of):
        uly, blk = lay.join(col, which, core_of)
        return {"uly": uly, "blk": blk}

    has_down, has_up = column > 0, column < last
    middle = has_down & has_up
    down, up = jnp.maximum(column - 1, 0), jnp.minimum(column + 1, last)
    targets = (device(down, chip, core), device(up, chip, core), device(column, chip, 1 - core))

    barrier = pltpu.get_barrier_semaphore()
    for rel in range(1, CHIPS):
        pl.semaphore_signal(
            barrier, inc=1, device_id=device(column, partner(chip, rel), core), device_id_type=MESH
        )
    pl.semaphore_signal(barrier, inc=1, device_id=targets[2], device_id_type=MESH)

    @pl.when(has_down)
    def _():
        pl.semaphore_signal(barrier, inc=1, device_id=targets[0], device_id_type=MESH)

    @pl.when(has_up)
    def _():
        pl.semaphore_signal(barrier, inc=1, device_id=targets[1], device_id_type=MESH)

    def cols(index, size):
        return pl.ds(pl.multiple_of(index * size, size), size)

    def slot_of(col, item, core_of):
        return col * GROUP + core_of * CHIPS + item

    here = slot_of(column, chip, core)

    def route(head, kind, rel):
        src, dst, size = (
            (k_ref, bufs[head][0].at[here], HD),
            (v_ref, bufs[head][1].at[here], HD),
            (q_ref, qbuf.at[head, rel], width),
        )[kind]
        return src.at[:, cols(partner(chip, rel) * heads + head, size)], dst

    def own(head, kind):
        src, dst = route(head, kind, 0)
        return pltpu.make_async_copy(src, dst, own_sem.at[head, kind])

    def plane(head, kind, rel):
        src, dst = route(head, kind, rel)
        return pltpu.make_async_remote_copy(
            src, dst, plane_send.at[head, kind, rel], plane_recv.at[head, kind, rel],
            device_id=device(column, partner(chip, rel), core), device_id_type=MESH,
        )

    for head in range(heads):
        for kind in range(3):
            own(head, kind).start()
    pl.semaphore_wait(barrier, CHIPS + has_down.astype(jnp.int32) + has_up.astype(jnp.int32))
    for head in range(heads):
        for kind in range(3):
            for rel in range(1, CHIPS):
                plane(head, kind, rel).start()

    def hop(head, kind, way, col, item, core_of):
        buf = bufs[head][kind]
        index = slot_of(col, item, core_of)
        return pltpu.make_async_remote_copy(
            buf.at[index], buf.at[index], relay_send.at[head, kind, way, col], recv.at[head, kind, index],
            device_id=targets[way], device_id_type=MESH,
        )

    def first(head):
        for kind in range(2):
            for rel in range(CHIPS):
                if rel == 0:
                    own(head, kind).wait()
                else:
                    plane(head, kind, rel).wait_recv()

                @pl.when(has_down)
                def _():
                    hop(head, kind, 0, column, partner(chip, rel), core).start()

                @pl.when(has_up)
                def _():
                    hop(head, kind, 1, column, partner(chip, rel), core).start()

                hop(head, kind, 2, column, partner(chip, rel), core).start()

    def relay(head):
        @pl.loop(1, lay.columns)
        def _(step):
            above, below = column + step, column - step
            for kind in range(2):
                @pl.loop(0, CHIPS)
                def _(item):
                    @pl.when((above <= last) & has_down)
                    def _():
                        hop(head, kind, 0, above, item, core).wait_recv()
                        hop(head, kind, 0, above, item, core).start()
                        hop(head, kind, 2, above, item, core).start()

                    @pl.when((below >= 0) & has_up)
                    def _():
                        hop(head, kind, 1, below, item, core).wait_recv()
                        hop(head, kind, 1, below, item, core).start()
                        hop(head, kind, 2, below, item, core).start()

    def finish(head, kind):
        @pl.loop(1, lay.columns)
        def _(step):
            above, below = column + step, column - step

            @pl.loop(0, CHIPS)
            def _(item):
                @pl.when((above <= last) & jnp.logical_not(has_down))
                def _():
                    hop(head, kind, 0, above, item, core).wait_recv()
                    hop(head, kind, 2, above, item, core).start()

                @pl.when((below >= 0) & jnp.logical_not(has_up))
                def _():
                    hop(head, kind, 1, below, item, core).wait_recv()
                    hop(head, kind, 2, below, item, core).start()

        @pl.loop(0, lay.columns)
        def _(col):
            @pl.loop(0, CHIPS)
            def _(item):
                hop(head, kind, 2, col, item, 1 - core).wait_recv()

    factor = math.log2(math.e) / math.sqrt(HD)

    def picked(buf, rel):
        uly, blk = lay.join(column, partner(chip, rel), core)
        block = blk * lay.n_uly + uly
        return jnp.concatenate([buf[lay.slot(live_ref[block, i])] for i in range(live)], axis=0)

    def weigh(head):
        own(head, 2).wait()
        for rel in range(1, CHIPS):
            plane(head, 2, rel).wait_recv()

        @pl.loop(0, CHIPS)
        def _(rel):
            queries = jnp.concatenate(
                [qbuf[head, rel, :, r * HD:(r + 1) * HD] for r in range(share)], axis=0
            )
            scores = lax.dot_general(
                queries, picked(bufs[head][0], rel), (((1,), (1,)), ((), ())),
                preferred_element_type=jnp.float32,
            )
            row_max = jnp.max(scores, axis=1, keepdims=True)
            weights = jnp.exp2((scores - row_max) * factor)
            total = jnp.sum(weights, axis=1, keepdims=True)
            lbuf[rel] = jnp.broadcast_to(total, lbuf.shape[1:])
            pbuf[rel] = weights.astype(jnp.bfloat16)

    def out_cols(head):
        return cols(chip * heads + head, width)

    def back(head, rel):
        return pltpu.make_async_remote_copy(
            obuf.at[head, rel], o_ref.at[:, out_cols(head)], o_send.at[head, rel], o_recv.at[head, rel],
            device_id=device(column, partner(chip, rel), core), device_id_type=MESH,
        )

    def attended(head, rel):
        product = jnp.dot(pbuf[rel], picked(bufs[head][1], rel), preferred_element_type=jnp.float32)
        result = (product / lbuf[rel]).astype(jnp.bfloat16)
        rows = result.shape[0] // share
        return jnp.concatenate([result[r * rows:(r + 1) * rows] for r in range(share)], axis=1)

    def attend(head):
        @pl.loop(0, CHIPS - 1)
        def _(step):
            rel = CHIPS - 1 - step
            obuf[head, rel] = attended(head, rel)

            @pl.when(step > 0)
            def _():
                back(head, rel + 1).start()

        o_ref[:, out_cols(head)] = attended(head, 0)
        back(head, 1).start()

    first(0)

    @pl.when(jnp.logical_not(middle))
    def _():
        for head in range(1, heads):
            first(head)

    relay(0)

    @pl.when(middle)
    def _():
        for head in range(1, heads):
            first(head)

    for head in range(1, heads):
        relay(head)
    for head in range(heads):
        finish(head, 0)
        weigh(head)
        finish(head, 1)
        attend(head)

    for head in range(heads):
        for kind in range(3):
            for rel in range(1, CHIPS):
                plane(head, kind, rel).wait_send()

    def sent(head, kind, way, col):
        buf = bufs[head][kind].at[pl.ds(slot_of(col, 0, core), CHIPS)]
        pltpu.make_async_copy(buf, buf, relay_send.at[head, kind, way, col]).wait()

    @pl.loop(0, lay.columns)
    def _(col):
        for head in range(heads):
            for kind in range(2):
                @pl.when((col >= column) & has_down)
                def _():
                    sent(head, kind, 0, col)

                @pl.when((col <= column) & has_up)
                def _():
                    sent(head, kind, 1, col)

                sent(head, kind, 2, col)

    for head in range(heads):
        for rel in range(1, CHIPS):
            back(head, rel).wait()


def solution(mesh):
    lay = Layout(mesh.shape["uly"], mesh.shape["blk"])

    def body(queries, keys, values, live_blocks):
        rows, hidden = queries.shape
        heads = keys.shape[1] // HD // CHIPS
        width = hidden // CHIPS // heads
        share = width // HD
        slots = lay.columns * GROUP
        keys_seen = live_blocks.shape[1] * rows
        bf16, f32 = jnp.bfloat16, jnp.float32
        dma = pltpu.SemaphoreType.DMA
        vmem = pl.BlockSpec(memory_space=pltpu.VMEM)

        def call(*refs):
            kernel(lay, *refs)

        return pl.pallas_call(
            call,
            out_shape=jax.ShapeDtypeStruct((rows, hidden), bf16),
            in_specs=[pl.BlockSpec(memory_space=pltpu.SMEM), vmem, vmem, vmem],
            out_specs=vmem,
            scratch_shapes=[
                pltpu.VMEM((heads, CHIPS, rows, width), bf16),
                *[pltpu.VMEM((slots, rows, HD), bf16) for _ in range(4)],
                pltpu.VMEM((CHIPS, rows * share, keys_seen), bf16),
                pltpu.VMEM((CHIPS, rows * share, HD), f32),
                pltpu.VMEM((heads, CHIPS, rows, width), bf16),
                dma((heads, 3, CHIPS)),
                dma((heads, 3, CHIPS)),
                dma((heads, 3)),
                dma((heads, 2, 3, lay.columns)),
                dma((heads, 2, slots)),
                dma((heads, CHIPS)),
                dma((heads, CHIPS)),
            ],
            compiler_params=pltpu.CompilerParams(
                collective_id=0, has_side_effects=True, vmem_limit_bytes=56 * 2**20
            ),
            name="group_attention",
        )(live_blocks, queries, keys, values)

    spec = P(("blk", "uly"), None)
    return jax.shard_map(
        body, mesh=mesh, in_specs=(spec, spec, spec, P()), out_specs=spec, check_vma=False
    )
```

```python
import math

import jax
import jax.numpy as jnp
from jax import lax
from jax.experimental import pallas as pl
from jax.experimental.pallas import tpu as pltpu
from jax.sharding import PartitionSpec as P

HD = 128
CORES = 2
SIDE = 2
CHIPS = SIDE * SIDE
GROUP = CHIPS * CORES
MESH = pl.DeviceIdType.MESH


class Layout:
    def __init__(self, n_uly, n_blk):
        self.n_uly = n_uly
        self.nx = n_blk // CORES
        self.ny = 2 ** (int(math.log2(n_uly)) // 2)
        self.nz = n_uly // self.ny
        self.columns = n_uly * n_blk // GROUP

    def split(self, uly, blk):
        x, core = blk // CORES, blk % CORES
        z, y = uly // self.ny, uly % self.ny
        column = ((x // SIDE) * (self.ny // SIDE) + y // SIDE) * self.nz + z
        return column, (x % SIDE) * SIDE + y % SIDE, core

    def join(self, column, chip, core):
        z, square = column % self.nz, column // self.nz
        x = (square // (self.ny // SIDE)) * SIDE + chip // SIDE
        y = (square % (self.ny // SIDE)) * SIDE + chip % SIDE
        return z * self.ny + y, x * CORES + core

    def slot(self, block):
        column, chip, core = self.split(block % self.n_uly, block // self.n_uly)
        return column * GROUP + core * CHIPS + chip


def partner(chip, rel):
    a = (chip // 2 + rel // 2) % 2
    b = (chip % 2 + rel % 2) % 2
    return a * 2 + b


def kernel(lay, live_hbm, q_ref, k_ref, v_ref, o_ref,
           live_ref, live_sem, qbuf, ka, va, kb, vb, pbuf, lbuf, obuf,
           plane_send, plane_recv, own_sem, relay_send, recv, o_send, o_recv):
    heads = k_ref.shape[1] // HD // CHIPS
    width = q_ref.shape[1] // CHIPS // heads
    share = width // HD
    live = live_ref.shape[1]
    last = lay.columns - 1
    bufs = ((ka, va), (kb, vb))
    column, chip, core = lay.split(lax.axis_index("uly"), lax.axis_index("blk"))

    def device(col, which, core_of):
        uly, blk = lay.join(col, which, core_of)
        return {"uly": uly, "blk": blk}

    has_down, has_up = column > 0, column < last
    middle = has_down & has_up
    down, up = jnp.maximum(column - 1, 0), jnp.minimum(column + 1, last)
    targets = (device(down, chip, core), device(up, chip, core), device(column, chip, 1 - core))

    fetch = pltpu.make_async_copy(live_hbm, live_ref, live_sem)
    fetch.start()
    barrier = pltpu.get_barrier_semaphore()
    for rel in range(1, CHIPS):
        pl.semaphore_signal(
            barrier, inc=1, device_id=device(column, partner(chip, rel), core), device_id_type=MESH
        )
    pl.semaphore_signal(barrier, inc=1, device_id=targets[2], device_id_type=MESH)

    @pl.when(has_down)
    def _():
        pl.semaphore_signal(barrier, inc=1, device_id=targets[0], device_id_type=MESH)

    @pl.when(has_up)
    def _():
        pl.semaphore_signal(barrier, inc=1, device_id=targets[1], device_id_type=MESH)

    def cols(index, size):
        return pl.ds(pl.multiple_of(index * size, size), size)

    def slot_of(col, item, core_of):
        return col * GROUP + core_of * CHIPS + item

    here = slot_of(column, chip, core)

    def route(head, kind, rel):
        src, dst, size = (
            (k_ref, bufs[head][0].at[here], HD),
            (v_ref, bufs[head][1].at[here], HD),
            (q_ref, qbuf.at[head, rel], width),
        )[kind]
        return src.at[:, cols(partner(chip, rel) * heads + head, size)], dst

    def own(head, kind):
        src, dst = route(head, kind, 0)
        return pltpu.make_async_copy(src, dst, own_sem.at[head, kind])

    def plane(head, kind, rel):
        src, dst = route(head, kind, rel)
        return pltpu.make_async_remote_copy(
            src, dst, plane_send.at[head, kind, rel], plane_recv.at[head, kind, rel],
            device_id=device(column, partner(chip, rel), core), device_id_type=MESH,
        )

    for head in range(heads):
        for kind in range(3):
            own(head, kind).start()
    pl.semaphore_wait(barrier, CHIPS + has_down.astype(jnp.int32) + has_up.astype(jnp.int32))
    for head in range(heads):
        for kind in range(3):
            for rel in range(1, CHIPS):
                plane(head, kind, rel).start()

    def hop(head, kind, way, col, item, core_of):
        buf = bufs[head][kind]
        index = slot_of(col, item, core_of)
        return pltpu.make_async_remote_copy(
            buf.at[index], buf.at[index], relay_send.at[head, kind, way, col], recv.at[head, kind, index],
            device_id=targets[way], device_id_type=MESH,
        )

    def first(head):
        for kind in range(2):
            for rel in range(CHIPS):
                if rel == 0:
                    own(head, kind).wait()
                else:
                    plane(head, kind, rel).wait_recv()

                @pl.when(has_down)
                def _():
                    hop(head, kind, 0, column, partner(chip, rel), core).start()

                @pl.when(has_up)
                def _():
                    hop(head, kind, 1, column, partner(chip, rel), core).start()

                hop(head, kind, 2, column, partner(chip, rel), core).start()

    def relay(head):
        for kind in range(2):
            @pl.loop(1, lay.columns)
            def _(step):
                above, below = column + step, column - step

                @pl.loop(0, CHIPS)
                def _(item):
                    @pl.when((above <= last) & has_down)
                    def _():
                        hop(head, kind, 0, above, item, core).wait_recv()
                        hop(head, kind, 0, above, item, core).start()
                        hop(head, kind, 2, above, item, core).start()

                    @pl.when((below >= 0) & has_up)
                    def _():
                        hop(head, kind, 1, below, item, core).wait_recv()
                        hop(head, kind, 1, below, item, core).start()
                        hop(head, kind, 2, below, item, core).start()

    def finish(head, kind):
        @pl.loop(1, lay.columns)
        def _(step):
            above, below = column + step, column - step

            @pl.loop(0, CHIPS)
            def _(item):
                @pl.when((above <= last) & jnp.logical_not(has_down))
                def _():
                    hop(head, kind, 0, above, item, core).wait_recv()
                    hop(head, kind, 2, above, item, core).start()

                @pl.when((below >= 0) & jnp.logical_not(has_up))
                def _():
                    hop(head, kind, 1, below, item, core).wait_recv()
                    hop(head, kind, 2, below, item, core).start()

        @pl.loop(0, lay.columns)
        def _(col):
            @pl.loop(0, CHIPS)
            def _(item):
                hop(head, kind, 2, col, item, 1 - core).wait_recv()

    factor = math.log2(math.e) / math.sqrt(HD)

    def picked(buf, rel):
        uly, blk = lay.join(column, partner(chip, rel), core)
        block = blk * lay.n_uly + uly
        return jnp.concatenate([buf[lay.slot(live_ref[block, i])] for i in range(live)], axis=0)

    def weigh(head):
        own(head, 2).wait()
        for rel in range(1, CHIPS):
            plane(head, 2, rel).wait_recv()

        @pl.loop(0, CHIPS)
        def _(rel):
            queries = jnp.concatenate(
                [qbuf[head, rel, :, r * HD:(r + 1) * HD] for r in range(share)], axis=0
            )
            scores = lax.dot_general(
                queries, picked(bufs[head][0], rel), (((1,), (1,)), ((), ())),
                preferred_element_type=jnp.float32,
            )
            row_max = jnp.max(scores, axis=1, keepdims=True)
            weights = jnp.exp2((scores - row_max) * factor)
            total = jnp.sum(weights, axis=1, keepdims=True)
            lbuf[rel] = jnp.broadcast_to(total, lbuf.shape[1:])
            pbuf[rel] = weights.astype(jnp.bfloat16)

    def out_cols(head):
        return cols(chip * heads + head, width)

    def back(head, rel):
        return pltpu.make_async_remote_copy(
            obuf.at[head, rel], o_ref.at[:, out_cols(head)], o_send.at[head, rel], o_recv.at[head, rel],
            device_id=device(column, partner(chip, rel), core), device_id_type=MESH,
        )

    def attended(head, rel):
        product = jnp.dot(pbuf[rel], picked(bufs[head][1], rel), preferred_element_type=jnp.float32)
        result = (product / lbuf[rel]).astype(jnp.bfloat16)
        rows = result.shape[0] // share
        return jnp.concatenate([result[r * rows:(r + 1) * rows] for r in range(share)], axis=1)

    def attend(head):
        @pl.loop(0, CHIPS - 1)
        def _(step):
            rel = CHIPS - 1 - step
            obuf[head, rel] = attended(head, rel)

            @pl.when(step > 0)
            def _():
                back(head, rel + 1).start()

        o_ref[:, out_cols(head)] = attended(head, 0)
        back(head, 1).start()

    first(0)
    fetch.wait()

    @pl.when(jnp.logical_not(middle))
    def _():
        for head in range(1, heads):
            first(head)

    relay(0)

    @pl.when(middle)
    def _():
        for head in range(1, heads):
            first(head)

    for head in range(heads):
        if head > 0:
            relay(head)
        finish(head, 0)
        weigh(head)
        finish(head, 1)
        attend(head)

    for head in range(heads):
        for kind in range(3):
            for rel in range(1, CHIPS):
                plane(head, kind, rel).wait_send()

    def sent(head, kind, way, col):
        buf = bufs[head][kind].at[pl.ds(slot_of(col, 0, core), CHIPS)]
        pltpu.make_async_copy(buf, buf, relay_send.at[head, kind, way, col]).wait()

    @pl.loop(0, lay.columns)
    def _(col):
        for head in range(heads):
            for kind in range(2):
                @pl.when((col >= column) & has_down)
                def _():
                    sent(head, kind, 0, col)

                @pl.when((col <= column) & has_up)
                def _():
                    sent(head, kind, 1, col)

                sent(head, kind, 2, col)

    for head in range(heads):
        for rel in range(1, CHIPS):
            back(head, rel).wait()


def solution(mesh):
    lay = Layout(mesh.shape["uly"], mesh.shape["blk"])

    def body(queries, keys, values, live_blocks):
        rows, hidden = queries.shape
        heads = keys.shape[1] // HD // CHIPS
        width = hidden // CHIPS // heads
        share = width // HD
        slots = lay.columns * GROUP
        keys_seen = live_blocks.shape[1] * rows
        bf16, f32 = jnp.bfloat16, jnp.float32
        dma = pltpu.SemaphoreType.DMA

        def call(*refs):
            kernel(lay, *refs)

        return pl.pallas_call(
            call,
            out_shape=jax.ShapeDtypeStruct((rows, hidden), bf16),
            in_specs=[pl.BlockSpec(memory_space=pl.ANY)] * 4,
            out_specs=pl.BlockSpec(memory_space=pltpu.VMEM),
            scratch_shapes=[
                pltpu.SMEM(live_blocks.shape, live_blocks.dtype),
                dma,
                pltpu.VMEM((heads, CHIPS, rows, width), bf16),
                *[pltpu.VMEM((slots, rows, HD), bf16) for _ in range(4)],
                pltpu.VMEM((CHIPS, rows * share, keys_seen), bf16),
                pltpu.VMEM((CHIPS, rows * share, HD), f32),
                pltpu.VMEM((heads, CHIPS, rows, width), bf16),
                dma((heads, 3, CHIPS)),
                dma((heads, 3, CHIPS)),
                dma((heads, 3)),
                dma((heads, 2, 3, lay.columns)),
                dma((heads, 2, slots)),
                dma((heads, CHIPS)),
                dma((heads, CHIPS)),
            ],
            compiler_params=pltpu.CompilerParams(
                collective_id=0, has_side_effects=True, vmem_limit_bytes=56 * 2**20
            ),
            name="group_attention",
        )(live_blocks, queries, keys, values)

    spec = P(("blk", "uly"), None)
    return jax.shard_map(
        body, mesh=mesh, in_specs=(spec, spec, spec, P()), out_specs=spec, check_vma=False
    )
```

```python
import math

import jax
import jax.numpy as jnp
from jax import lax
from jax.experimental import pallas as pl
from jax.experimental.pallas import tpu as pltpu
from jax.sharding import PartitionSpec as P

HD = 128
CORES = 2
SIDE = 2
CHIPS = SIDE * SIDE
GROUP = CHIPS * CORES
MESH = pl.DeviceIdType.MESH


class Layout:
    def __init__(self, n_uly, n_blk):
        self.n_uly = n_uly
        self.nx = n_blk // CORES
        self.ny = 2 ** (int(math.log2(n_uly)) // 2)
        self.nz = n_uly // self.ny
        self.columns = n_uly * n_blk // GROUP

    def split(self, uly, blk):
        x, core = blk // CORES, blk % CORES
        z, y = uly // self.ny, uly % self.ny
        column = ((x // SIDE) * (self.ny // SIDE) + y // SIDE) * self.nz + z
        return column, (x % SIDE) * SIDE + y % SIDE, core

    def join(self, column, chip, core):
        z, square = column % self.nz, column // self.nz
        x = (square // (self.ny // SIDE)) * SIDE + chip // SIDE
        y = (square % (self.ny // SIDE)) * SIDE + chip % SIDE
        return z * self.ny + y, x * CORES + core

    def slot(self, block):
        column, chip, core = self.split(block % self.n_uly, block // self.n_uly)
        return column * GROUP + core * CHIPS + chip


def partner(chip, rel):
    a = (chip // 2 + rel // 2) % 2
    b = (chip % 2 + rel % 2) % 2
    return a * 2 + b


def kernel(lay, live_hbm, q_ref, k_ref, v_ref, o_ref,
           live_ref, live_sem, qbuf, ka, va, kb, vb, pbuf, lbuf, obuf,
           plane_send, plane_recv, own_sem, relay_send, recv, o_send, o_recv):
    heads = k_ref.shape[1] // HD // CHIPS
    width = q_ref.shape[1] // CHIPS // heads
    share = width // HD
    live = live_ref.shape[1]
    last = lay.columns - 1
    bufs = ((ka, va), (kb, vb))
    column, chip, core = lay.split(lax.axis_index("uly"), lax.axis_index("blk"))

    def device(col, which, core_of):
        uly, blk = lay.join(col, which, core_of)
        return {"uly": uly, "blk": blk}

    has_down, has_up = column > 0, column < last
    middle = has_down & has_up
    down, up = jnp.maximum(column - 1, 0), jnp.minimum(column + 1, last)
    targets = (device(down, chip, core), device(up, chip, core), device(column, chip, 1 - core))

    fetch = pltpu.make_async_copy(live_hbm, live_ref, live_sem)
    fetch.start()
    barrier = pltpu.get_barrier_semaphore()
    for rel in range(1, CHIPS):
        pl.semaphore_signal(
            barrier, inc=1, device_id=device(column, partner(chip, rel), core), device_id_type=MESH
        )
    pl.semaphore_signal(barrier, inc=1, device_id=targets[2], device_id_type=MESH)

    @pl.when(has_down)
    def _():
        pl.semaphore_signal(barrier, inc=1, device_id=targets[0], device_id_type=MESH)

    @pl.when(has_up)
    def _():
        pl.semaphore_signal(barrier, inc=1, device_id=targets[1], device_id_type=MESH)

    def cols(index, size):
        return pl.ds(pl.multiple_of(index * size, size), size)

    def slot_of(col, item, core_of):
        return col * GROUP + core_of * CHIPS + item

    here = slot_of(column, chip, core)

    def route(head, kind, rel):
        src, dst, size = (
            (k_ref, bufs[head][0].at[here], HD),
            (v_ref, bufs[head][1].at[here], HD),
            (q_ref, qbuf.at[head, rel], width),
        )[kind]
        return src.at[:, cols(partner(chip, rel) * heads + head, size)], dst

    def own(head, kind):
        src, dst = route(head, kind, 0)
        return pltpu.make_async_copy(src, dst, own_sem.at[head, kind])

    def plane(head, kind, rel):
        src, dst = route(head, kind, rel)
        return pltpu.make_async_remote_copy(
            src, dst, plane_send.at[head, kind, rel], plane_recv.at[head, kind, rel],
            device_id=device(column, partner(chip, rel), core), device_id_type=MESH,
        )

    for head in range(heads):
        for kind in range(3):
            own(head, kind).start()
    pl.semaphore_wait(barrier, CHIPS + has_down.astype(jnp.int32) + has_up.astype(jnp.int32))
    for head in range(heads):
        for kind in range(3):
            for rel in range(1, CHIPS):
                plane(head, kind, rel).start()

    def hop(head, kind, way, col, item, core_of):
        buf = bufs[head][kind]
        index = slot_of(col, item, core_of)
        return pltpu.make_async_remote_copy(
            buf.at[index], buf.at[index], relay_send.at[head, kind, way, col], recv.at[head, kind, index],
            device_id=targets[way], device_id_type=MESH,
        )

    def first(head):
        for kind in range(2):
            for rel in range(CHIPS):
                if rel == 0:
                    own(head, kind).wait()
                else:
                    plane(head, kind, rel).wait_recv()

                @pl.when(has_down)
                def _():
                    hop(head, kind, 0, column, partner(chip, rel), core).start()

                @pl.when(has_up)
                def _():
                    hop(head, kind, 1, column, partner(chip, rel), core).start()

                hop(head, kind, 2, column, partner(chip, rel), core).start()

    def relay(head):
        for kind in range(2):
            @pl.loop(1, lay.columns)
            def _(step):
                above, below = column + step, column - step

                @pl.loop(0, CHIPS)
                def _(item):
                    @pl.when((above <= last) & has_down)
                    def _():
                        hop(head, kind, 0, above, item, core).wait_recv()
                        hop(head, kind, 0, above, item, core).start()
                        hop(head, kind, 2, above, item, core).start()

                    @pl.when((below >= 0) & has_up)
                    def _():
                        hop(head, kind, 1, below, item, core).wait_recv()
                        hop(head, kind, 1, below, item, core).start()
                        hop(head, kind, 2, below, item, core).start()

    def finish(head, kind):
        @pl.loop(1, lay.columns)
        def _(step):
            above, below = column + step, column - step

            @pl.loop(0, CHIPS)
            def _(item):
                @pl.when((above <= last) & jnp.logical_not(has_down))
                def _():
                    hop(head, kind, 0, above, item, core).wait_recv()
                    hop(head, kind, 2, above, item, core).start()

                @pl.when((below >= 0) & jnp.logical_not(has_up))
                def _():
                    hop(head, kind, 1, below, item, core).wait_recv()
                    hop(head, kind, 2, below, item, core).start()

        @pl.loop(0, lay.columns)
        def _(col):
            @pl.loop(0, CHIPS)
            def _(item):
                hop(head, kind, 2, col, item, 1 - core).wait_recv()

    factor = math.log2(math.e) / math.sqrt(HD)

    def picked(buf, rel):
        uly, blk = lay.join(column, partner(chip, rel), core)
        block = blk * lay.n_uly + uly
        return jnp.concatenate([buf[lay.slot(live_ref[block, i])] for i in range(live)], axis=0)

    def weigh(head):
        own(head, 2).wait()
        for rel in range(1, CHIPS):
            plane(head, 2, rel).wait_recv()

        @pl.loop(0, CHIPS)
        def _(rel):
            queries = jnp.concatenate(
                [qbuf[head, rel, :, r * HD:(r + 1) * HD] for r in range(share)], axis=0
            )
            scores = lax.dot_general(
                queries, picked(bufs[head][0], rel), (((1,), (1,)), ((), ())),
                preferred_element_type=jnp.float32,
            )
            row_max = jnp.max(scores, axis=1, keepdims=True)
            weights = jnp.exp2((scores - row_max) * factor)
            total = jnp.sum(weights, axis=1, keepdims=True)
            lbuf[rel] = jnp.broadcast_to(total, lbuf.shape[1:])
            pbuf[rel] = weights.astype(jnp.bfloat16)

    def halves(part):
        return pl.ds(part * (width // 2), width // 2)

    def out_cols(head, part):
        return cols((chip * heads + head) * 2 + part, width // 2)

    def back(head, rel, part):
        return pltpu.make_async_remote_copy(
            obuf.at[head, rel, :, halves(part)], o_ref.at[:, out_cols(head, part)],
            o_send.at[head, rel, part], o_recv.at[head, rel, part],
            device_id=device(column, partner(chip, rel), core), device_id_type=MESH,
        )

    def attended(rel, part, values_here):
        rows = pbuf.shape[1] // share
        picks = pl.ds(part * (pbuf.shape[1] // 2), pbuf.shape[1] // 2)
        product = jnp.dot(pbuf[rel, picks, :], values_here, preferred_element_type=jnp.float32)
        result = (product / lbuf[rel, picks, :]).astype(jnp.bfloat16)
        return jnp.concatenate([result[r * rows:(r + 1) * rows] for r in range(share // 2)], axis=1)

    def attend(head):
        @pl.loop(0, CHIPS - 1)
        def _(step):
            rel = CHIPS - 1 - step
            values_here = picked(bufs[head][1], rel)
            for part in range(2):
                obuf[head, rel, :, halves(part)] = attended(rel, part, values_here)
                if part == 1:
                    back(head, rel, 0).start()
                else:
                    @pl.when(step > 0)
                    def _():
                        back(head, rel + 1, 1).start()

        values_here = picked(bufs[head][1], 0)
        for part in range(2):
            o_ref[:, out_cols(head, part)] = attended(0, part, values_here)
            if part == 0:
                back(head, 1, 1).start()

    first(0)
    fetch.wait()

    @pl.when(jnp.logical_not(middle))
    def _():
        for head in range(1, heads):
            first(head)

    relay(0)

    @pl.when(middle)
    def _():
        for head in range(1, heads):
            first(head)

    for head in range(heads):
        if head > 0:
            relay(head)
        finish(head, 0)
        weigh(head)
        finish(head, 1)
        attend(head)

    for head in range(heads):
        for kind in range(3):
            for rel in range(1, CHIPS):
                plane(head, kind, rel).wait_send()

    def sent(head, kind, way, col):
        buf = bufs[head][kind].at[pl.ds(slot_of(col, 0, core), CHIPS)]
        pltpu.make_async_copy(buf, buf, relay_send.at[head, kind, way, col]).wait()

    @pl.loop(0, lay.columns)
    def _(col):
        for head in range(heads):
            for kind in range(2):
                @pl.when((col >= column) & has_down)
                def _():
                    sent(head, kind, 0, col)

                @pl.when((col <= column) & has_up)
                def _():
                    sent(head, kind, 1, col)

                sent(head, kind, 2, col)

    for head in range(heads):
        for rel in range(1, CHIPS):
            for part in range(2):
                back(head, rel, part).wait()


def solution(mesh):
    lay = Layout(mesh.shape["uly"], mesh.shape["blk"])

    def body(queries, keys, values, live_blocks):
        rows, hidden = queries.shape
        heads = keys.shape[1] // HD // CHIPS
        width = hidden // CHIPS // heads
        share = width // HD
        slots = lay.columns * GROUP
        keys_seen = live_blocks.shape[1] * rows
        bf16, f32 = jnp.bfloat16, jnp.float32
        dma = pltpu.SemaphoreType.DMA

        def call(*refs):
            kernel(lay, *refs)

        return pl.pallas_call(
            call,
            out_shape=jax.ShapeDtypeStruct((rows, hidden), bf16),
            in_specs=[pl.BlockSpec(memory_space=pl.ANY)] * 4,
            out_specs=pl.BlockSpec(memory_space=pltpu.VMEM),
            scratch_shapes=[
                pltpu.SMEM(live_blocks.shape, live_blocks.dtype),
                dma,
                pltpu.VMEM((heads, CHIPS, rows, width), bf16),
                *[pltpu.VMEM((slots, rows, HD), bf16) for _ in range(4)],
                pltpu.VMEM((CHIPS, rows * share, keys_seen), bf16),
                pltpu.VMEM((CHIPS, rows * share, HD), f32),
                pltpu.VMEM((heads, CHIPS, rows, width), bf16),
                dma((heads, 3, CHIPS)),
                dma((heads, 3, CHIPS)),
                dma((heads, 3)),
                dma((heads, 2, 3, lay.columns)),
                dma((heads, 2, slots)),
                dma((heads, CHIPS, 2)),
                dma((heads, CHIPS, 2)),
            ],
            compiler_params=pltpu.CompilerParams(
                collective_id=0, has_side_effects=True, vmem_limit_bytes=56 * 2**20
            ),
            name="group_attention",
        )(live_blocks, queries, keys, values)

    spec = P(("blk", "uly"), None)
    return jax.shard_map(
        body, mesh=mesh, in_specs=(spec, spec, spec, P()), out_specs=spec, check_vma=False
    )
```
